32 devices in a mesh: pipe: 2 (over core), node: 8 (over z, x), head: 2 (over y).
Axes of the slice: x: 2, y: 2, z: 4, core: 2. Of those that a mesh axis runs over, the one named last changes fastest.
Arguments:
- feats: bfloat16 [2, 1024, 2048], P(None, 'node', 'head'), may hold values from -20 to 20
- gain: float32 [2, 2048], P('pipe'), may hold values from 0.25 to 1.75
- w_qkv: bfloat16 [2, 3, 2048, 2048], P('pipe', None, 'node', 'head'), may hold values from -0.176776695 to 0.176776695
- w_out: bfloat16 [2, 2048, 2048], P('pipe', 'head', 'node'), may hold values from -1 to 1
- block_mask: int32 [2, 8, 8], replicated, may hold values from 0 to 1, as said below
Outputs:
- layers_out: bfloat16 [2, 2, 1024, 2048], P('pipe', None, 'node', 'head')
The draws below stay inside these ranges and needn't reach their ends.
Inputs may be any that keep to these rules, and one draw needn't show every extreme that they name: block_mask[m, b, b] = 1; block_mask[m, b, c] is 0 unless c = b or c = b xor 2^k with k one of L - 1, L // 2 and 0, where 2^L = 8.
All inputs are finite; a program needn't handle non-finite values.
Results may differ from the reference program's by a relative error of at most 0.023.
Values may be sent and summed in bfloat16 or wider, within the bound.
A program may use at most 64 MiB of HBM per device.

```python
import math
import jax
import jax.numpy as jnp
from jax import lax

D = 2048
HEADS = 16
HD = 128
BLOCK = 128
MICRO = 2
NBLK = 8
NODES = 1024
SEGMENTS = 2


def shared_signs(key):
    picks = jax.random.randint(jax.random.fold_in(key, 101), (D,), 0, 2)
    return picks.astype(jnp.float32) * 2.0 - 1.0


def draw_feats(key, part):
    signs = shared_signs(key)
    chosen = max(2, BLOCK // 32)
    spacing = BLOCK // chosen
    offset = jax.random.randint(jax.random.fold_in(key, 202), (MICRO, NBLK, 1), 0, spacing)
    places = jnp.arange(BLOCK, dtype=jnp.int32)[None, None, :]
    picked = (places - offset) % spacing == 0
    strength = jnp.exp(jax.random.uniform(jax.random.fold_in(key, 303), (MICRO, NBLK, BLOCK), jnp.float32, math.log(3.0), math.log(14.0)))
    lifted = jnp.where(picked, strength, 0.0).reshape(MICRO, NODES, 1)
    noise = jax.random.truncated_normal(jax.random.fold_in(key, 404), -6.0, 6.0, (MICRO, NODES, D), jnp.float32)
    return (lifted * signs[None, None, :] + noise).astype(jnp.bfloat16)


def draw_w_qkv(key, part):
    unit_dir = shared_signs(key) * D ** (-0.5)
    spread = D ** (-0.5)
    base = jax.random.truncated_normal(jax.random.fold_in(key, 505), -6.0, 6.0, (SEGMENTS, 3, D, D), jnp.float32) * spread
    column_bits = jax.random.randint(jax.random.fold_in(key, 606), (SEGMENTS, D), 0, 2)
    column_signs = column_bits.astype(jnp.float32) * 2.0 - 1.0
    head_strength = jnp.exp(jax.random.uniform(jax.random.fold_in(key, 707), (SEGMENTS, HEADS), jnp.float32, math.log(1.2), math.log(2.4)))
    amplitude = jnp.sqrt(head_strength * (180.0 * HD ** 0.5 / D))
    columns = column_signs * jnp.repeat(amplitude, HD, axis=1) * HD ** (-0.5)
    lifted = unit_dir[None, :, None] * columns[:, None, :]
    select = jnp.array([1.0, 1.0, 0.0], dtype=jnp.float32)
    return (base + select[None, :, None, None] * lifted[:, None, :, :]).astype(jnp.bfloat16)


def draw_block_mask(key, part):
    rows = jnp.arange(NBLK, dtype=jnp.int32)[:, None]
    cols = jnp.arange(NBLK, dtype=jnp.int32)[None, :]
    width = NBLK.bit_length() - 1
    near = jnp.zeros((NBLK, NBLK), dtype=bool)
    for bit in [width - 1, width // 2, 0]:
        near = near | (jnp.bitwise_xor(rows, 1 << bit) == cols)
    coin = jax.random.randint(key, (MICRO, NBLK, NBLK), 0, 4) > 0
    ones = jnp.where(rows == cols, True, near[None] & coin)
    return jnp.where(ones, 1, 0).astype(jnp.int32)


def steps_of(key, shape, cuts, smallest, top_value):
    level, own = 1.0, jax.random.fold_in(key, 6)
    for position, parts in cuts:
        steps = jnp.exp(jax.random.uniform(jax.random.fold_in(own, position), (parts,), jnp.float32, smallest / len(cuts), top_value / len(cuts)))
        level = level * jnp.repeat(steps, shape[position] // parts).reshape([-1 if axis == position else 1 for axis in range(len(shape))])
    return level


def normal_values(own_key, shape, deviation, limit, cuts=(), kind=jnp.bfloat16):
    entries = deviation * jax.random.normal(own_key, shape, jnp.float32)
    if cuts:
        entries = entries * steps_of(own_key, shape, cuts, -0.22, 0.18)
    return jnp.clip(entries, -limit, limit).astype(kind)


def setup_inputs(seed: int = 0) -> dict:
    seeds = jax.random.split(jax.random.key(seed), 6)
    return {
        "feats": draw_feats(jax.random.fold_in(seeds[5], 71), 0),
        "gain": jnp.clip(1.0 + 0.15 * jax.random.normal(seeds[1], (SEGMENTS, D), jnp.float32), 0.25, 1.75),
        "w_qkv": draw_w_qkv(jax.random.fold_in(seeds[5], 71), 0),
        "w_out": normal_values(seeds[3], (SEGMENTS, D, D), (D // 64) ** -0.5, 1.0, ((0, 2), (1, 2), (2, 8))),
        "block_mask": draw_block_mask(jax.random.fold_in(seeds[5], 71), 0),
    }


EPS = 1e-06
NEG = -1e+30

def partner_bits():
    width = NBLK.bit_length() - 1
    return [width - 1, width // 2, 0]

def layer(x, gain_row, w_qkv_s, w_out_s, mask_m):
    xf = x.astype(jnp.float32)
    inv = lax.rsqrt(lax.optimization_barrier(jnp.mean(xf * xf, axis=-1, keepdims=True)) + EPS)
    normed = (xf * inv * gain_row).astype(jnp.bfloat16)
    query = jnp.dot(normed, w_qkv_s[0], preferred_element_type=jnp.float32).astype(jnp.bfloat16)
    key = jnp.dot(normed, w_qkv_s[1], preferred_element_type=jnp.float32).astype(jnp.bfloat16)
    value = jnp.dot(normed, w_qkv_s[2], preferred_element_type=jnp.float32).astype(jnp.bfloat16)
    q_blocks = query.reshape(NBLK, BLOCK, HEADS, HD)
    k_blocks = key.reshape(NBLK, BLOCK, HEADS, HD)
    v_blocks = value.reshape(NBLK, BLOCK, HEADS, HD)
    scale = 1.0 / HD ** 0.5

    def one_block(index):
        idx = [index] + [jnp.bitwise_xor(index, 1 << bit) for bit in partner_bits()]
        idx = jnp.stack(idx).astype(jnp.int32)
        flags = mask_m[index, idx] > 0
        keep = jnp.repeat(flags, BLOCK)
        kb = k_blocks[idx].reshape(len(partner_bits()) * BLOCK + BLOCK, HEADS, HD)
        vb = v_blocks[idx].reshape(len(partner_bits()) * BLOCK + BLOCK, HEADS, HD)
        qb = q_blocks[index]
        scores = jnp.einsum('qhd,khd->hqk', qb.astype(jnp.float32), kb.astype(jnp.float32)) * scale
        scores = jnp.where(keep[None, None, :], scores, NEG)
        top = lax.optimization_barrier(jnp.max(scores, axis=-1, keepdims=True))
        expo = jnp.where(keep[None, None, :], jnp.exp(scores - top), 0.0)
        total = lax.optimization_barrier(jnp.sum(expo, axis=-1))
        weights = expo.astype(jnp.bfloat16)
        summed = jnp.einsum('hqk,khd->hqd', weights.astype(jnp.float32), vb.astype(jnp.float32))
        out = summed / total[..., None]
        return jnp.transpose(out, (1, 0, 2)).reshape(BLOCK, D).astype(jnp.bfloat16)
    attended = lax.map(one_block, jnp.arange(NBLK, dtype=jnp.int32)).reshape(NODES, D)
    projected = jnp.dot(attended, w_out_s, preferred_element_type=jnp.float32)
    return (xf + projected).astype(jnp.bfloat16)

def reference(feats, gain, w_qkv, w_out, block_mask):
    first = []
    second = []
    for micro in range(MICRO):
        mid = layer(feats[micro], gain[0], w_qkv[0], w_out[0], block_mask[micro])
        first.append(mid)
        second.append(layer(mid, gain[1], w_qkv[1], w_out[1], block_mask[micro]))
    return jnp.stack([jnp.stack(first), jnp.stack(second)])
```

```python
import functools
import jax
import jax.numpy as jnp
from jax import lax
from jax.experimental import pallas as pl
from jax.experimental.pallas import tpu as pltpu
from jax.sharding import PartitionSpec as P

HD = 128
MICRO = 2


EPS = 1e-06
NEG = -1e30


def from_partner(block, axis, apart):
    count = lax.axis_size(axis)
    route = []
    for low in range(count):
        high = low | 1 << apart
        if high != low and high < count:
            route += [(low, high), (high, low)]
    return lax.ppermute(block, axis, route)


def from_behind(value, axis, steps):
    count = lax.axis_size(axis)
    first, last = (max(0, -steps), min(count, count - steps))
    return lax.ppermute(value, axis, [(source, source + steps) for source in range(first, last)])


def partial_attend(query, key, value, keep):
    rows = query.shape[0]
    groups = query.shape[1] // HD
    q_heads = query.reshape(rows, groups, HD)
    k_heads = key.reshape(key.shape[0], groups, HD)
    v_heads = value.reshape(value.shape[0], groups, HD)
    scores = jnp.einsum("qhd,khd->hqk", q_heads, k_heads, preferred_element_type=jnp.float32) * (
        1.0 / HD**0.5
    )
    scores = jnp.where(keep[None, None, :], scores, NEG)
    top = jnp.max(scores, axis=-1)
    expo = jnp.where(keep[None, None, :], jnp.exp(scores - top[..., None]), 0.0)
    total = jnp.sum(expo, axis=-1)
    summed = jnp.einsum(
        "hqk,khd->hqd", expo.astype(jnp.bfloat16), v_heads, preferred_element_type=jnp.float32
    )
    return (summed, top, total)


def finish(summed, total):
    out = summed / total[..., None]
    rows = out.shape[1]
    return jnp.transpose(out, (1, 0, 2)).reshape(rows, -1).astype(jnp.bfloat16)


def local_any(feats, gain, w_qkv, w_out, block_mask):
    segment = lax.axis_index("pipe")
    me = lax.axis_index("node")
    width = lax.axis_size("node").bit_length() - 1
    bit_list = [width - 1, width // 2, 0]
    qkv_whole, out_whole = (
        lax.all_gather(w_qkv, "node", axis=2, tiled=True),
        lax.all_gather(w_out, "node", axis=2, tiled=True),
    )
    w_query = qkv_whole[0, 0]
    w_key = qkv_whole[0, 1]
    w_value = qkv_whole[0, 2]
    w_proj = out_whole[0]
    gain_row = gain[0]
    rows = feats.shape[1]
    carried = jnp.zeros_like(feats[0])
    results = []
    for tick in range(MICRO + 1):
        micro = jnp.clip(tick - segment, 0, MICRO - 1)
        fresh = feats[min(tick, MICRO - 1)]
        inputs = jnp.where(segment == 0, fresh, carried)
        whole = lax.all_gather(inputs, "head", axis=1, tiled=True)
        xf = whole.astype(jnp.float32)
        inv = lax.rsqrt(jnp.mean(xf * xf, axis=-1, keepdims=True) + EPS)
        normed = (xf * inv * gain_row).astype(jnp.bfloat16)
        query = jnp.dot(normed, w_query, preferred_element_type=jnp.float32).astype(jnp.bfloat16)
        key = jnp.dot(normed, w_key, preferred_element_type=jnp.float32).astype(jnp.bfloat16)
        value = jnp.dot(normed, w_value, preferred_element_type=jnp.float32).astype(jnp.bfloat16)
        mask_rows = lax.dynamic_index_in_dim(block_mask, micro, 0, keepdims=False)
        own_flag = mask_rows[me, me] > 0
        key_list = [key]
        value_list = [value]
        flag_list = [own_flag]
        for bit in bit_list:
            far_key, far_value = from_partner((key, value), "node", bit)
            key_list.append(far_key)
            value_list.append(far_value)
            flag_list.append(mask_rows[me, jnp.bitwise_xor(me, 1 << bit)] > 0)
        keep = jnp.repeat(jnp.stack(flag_list), rows)
        summed, top, total = partial_attend(
            query, jnp.concatenate(key_list, 0), jnp.concatenate(value_list, 0), keep
        )
        attended = finish(summed, total)
        terms = jnp.dot(attended, w_proj, preferred_element_type=jnp.float32)
        reduced = lax.psum_scatter(
            terms.astype(jnp.bfloat16), "head", scatter_dimension=1, tiled=True
        ).astype(jnp.float32)
        output = (inputs.astype(jnp.float32) + reduced).astype(jnp.bfloat16)
        results.append(output)
        if tick < MICRO:
            carried = from_behind(output, "pipe", 1)
    first = jnp.where(segment == 0, results[0], results[1])
    second = jnp.where(segment == 0, results[1], results[2])
    return jnp.stack([first, second])[None]


MESH_ID = pl.DeviceIdType.MESH
ANY = pl.BlockSpec(memory_space=pl.ANY)
PAIR = 2 * HD
KEY, QUERY, VALUE = 1, 0, 2


def place():
    core, node, y = lax.axis_index("pipe"), lax.axis_index("node"), lax.axis_index("head")
    return core, lax.rem(node, 2), y, lax.div(node, 2)


def dev(core, x, y, z):
    return (core, z * 2 + x, y)


def z_apart(z, d):
    if d == 0:
        return z
    if d == 1:
        return z + 1 - 2 * lax.rem(z, 2)
    if d == 2:
        return z + 2 - 4 * lax.div(z, 2)
    return 3 - z


def remote(src, dst, send, recv, target):
    return pltpu.make_async_remote_copy(
        src_ref=src, dst_ref=dst, send_sem=send, recv_sem=recv, device_id=target, device_id_type=MESH_ID
    )


def greet(peers):
    barrier = pltpu.get_barrier_semaphore()
    for peer in peers:
        pl.semaphore_signal(barrier, inc=1, device_id=peer, device_id_type=MESH_ID)
    pl.semaphore_wait(barrier, len(peers))


def relay_kernel(
    feats, gain, w_qkv, w_out, mask, out,
    xg, normed, gains, wq, wo, q_ref, k_ref, v_ref, e_ref, t_ref, attg, own_part, send_part, recv_part,
    rest, midg, fin, snd, rcv, w_sem, o_sem, f_sem, loc,
):
    core, x, y, z = place()
    zh, zl = lax.div(z, 2), lax.rem(z, 2)
    half = core + zh - 2 * core * zh
    rows, wide = feats.shape[1], feats.shape[2]
    depth = w_qkv.shape[2]
    tile = 2 * zl + x
    pair = 4 * y + tile
    sibling, over = dev(1 - core, x, y, z), z_apart(z, 2)
    partner = {"x": dev(core, 1 - x, y, z), "y": dev(core, x, 1 - y, z), "z": dev(core, x, y, z_apart(z, 1))}
    greet(
        [
            dev(cc, xx, y, z_apart(z, d))
            for d in range(4)
            for xx in (x, 1 - x)
            for cc in (core, 1 - core)
        ][1:]
        + [partner["y"]]
    )
    names, sent, local = {}, [], []

    def arrival(key):
        return rcv.at[names.setdefault(key, len(names))]

    def make(src, dst, sem, target):
        copy = remote(src, dst, snd.at[len(sent)], sem, target)
        sent.append((copy, None))
        return copy

    def push(src, dst, sem, target, when=None):
        copy = remote(src, dst, snd.at[len(sent)], sem, target)
        sent.append((copy, when))
        if when is None:
            copy.start()
        else:
            pl.when(when)(copy.start)

    def arrive(dst, sem):
        remote(dst, dst, snd.at[0], sem, sibling).wait_recv()

    def keep(src, dst, sem):
        copy = pltpu.make_async_copy(src, dst, sem)
        copy.start()
        local.append(copy)

    class Spread:
        def __init__(self, tag, order, region):
            self.tag, self.order, self.region = tag, order, region

        def at(self, off):
            return self.region(
                1 - x if "x" in off else x, 1 - y if "y" in off else y, 1 - zl if "z" in off else zl
            )

        def key(self, off):
            return arrival((self.tag, "".join(sorted(off))))

        def pass_on(self, off, dims):
            spot = self.at(off)
            for d in dims:
                push(spot, spot, self.key(off + d), partner[d])

        def start(self):
            self.pass_on("", self.order)

        def take(self, off):
            arrive(self.at(off), self.key(off))
            last = max(self.order.index(d) for d in off)
            self.pass_on(off, self.order[last + 1 :])

        def stage(self, i):
            d = self.order[i]
            for n in range(1 << i):
                self.take("".join(self.order[b] for b in range(i) if n >> b & 1) + d)

    def weight_copies(part):
        copies = []
        to = wq.at[core, part, pl.ds(pl.multiple_of((2 * z + x) * depth, depth), depth), :]
        for d in (2, 3, 1, 0):
            for xx in (1 - x, x):
                zz = z_apart(z, d)
                spot = pl.multiple_of((2 * lax.rem(zz, 2) + xx) * PAIR, PAIR)
                src = w_qkv.at[0, part, :, pl.ds(spot, PAIR)]
                if d == 0 and xx is x:
                    copies.append(pltpu.make_async_copy(src, to, w_sem.at[core, part]))
                else:
                    copies.append(make(src, to, w_sem.at[core, part], dev(core, xx, y, zz)))
        return copies

    weights = {part: weight_copies(part) for part in (KEY, QUERY, VALUE)}
    own_wo = wo.at[core, zh]
    wo_copies = [
        make(w_out.at[0], own_wo, o_sem.at[core, zh], dev(core, x, y, over)),
        make(w_out.at[0], own_wo, o_sem.at[core, zh], sibling),
        pltpu.make_async_copy(w_out.at[0], own_wo, o_sem.at[core, zh]),
    ]

    def begin(copies, section):
        @pl.when(core == section)
        def _():
            for copy in copies:
                copy.start()

    def await_weights(s, part):
        got = wq.at[s, part]
        arrive(got, w_sem.at[s, part])
        push(got, got, w_sem.at[s, part], sibling, core == s)

    def await_projection(s):
        arrive(wo.at[s, zh], o_sem.at[s, zh])
        got = wo.at[s, 1 - zh]
        arrive(got, o_sem.at[s, 1 - zh])
        push(got, got, o_sem.at[s, 1 - zh], sibling, core == s)

    own_spot = xg.at[y, pl.ds(pl.multiple_of(tile * rows, rows), rows), :]
    own_key = arrival("own")
    cross = make(feats.at[1 - zh], own_spot, own_key, dev(core, x, y, over))
    sent.pop()
    sent.append((cross, core == 1))
    pl.when(core == 1)(cross.start)
    pl.when(core == 0)(pltpu.make_async_copy(feats.at[zh], own_spot, own_key).start)
    push(gain, gains.at[core], arrival("gain"), sibling)
    keep(gain, gains.at[core], loc.at[0])
    arrive(own_spot, own_key)
    cut = rows // 2
    fs = [
        Spread(
            ("f", p), "zxy",
            lambda xx, yy, zz, p=p: xg.at[yy, pl.ds(pl.multiple_of((2 * zz + xx) * rows + p * cut, cut), cut), :],
        )
        for p in range(2)
    ]
    for f in fs:
        f.start()
    begin(weights[KEY], 0)
    for f in fs:
        f.stage(0)
    begin(weights[QUERY], 0)
    for f in fs:
        f.stage(1)
    begin(weights[VALUE] + wo_copies, 0)
    for f in fs:
        f.stage(2)
    arrive(gains.at[1 - core], arrival("gain"))
    local[0].wait()
    rest_copy = pltpu.make_async_copy(
        xg.at[y, :, pl.ds(pl.multiple_of(tile * PAIR, PAIR), PAIR)], rest, loc.at[1]
    )
    rest_copy.start()

    chunk = 16

    def normalize(load, width, count, s, first, length):
        def body(i, carry):
            span = pl.ds(pl.multiple_of(first + i * chunk, chunk), chunk)
            xs = [load(n, span).astype(jnp.float32) for n in range(count)]
            squares = functools.reduce(jnp.add, [jnp.sum(v * v, axis=-1, keepdims=True) for v in xs])
            inv = lax.rsqrt(squares * (1.0 / (width * count)) + EPS)
            for n, v in enumerate(xs):
                cols = slice(n * width, (n + 1) * width)
                normed[span, cols] = (v * inv * gains[s, :, cols]).astype(jnp.bfloat16)
            return carry

        lax.fori_loop(0, length // chunk, body, 0, unroll=2)

    def project(s, part, span):
        return jnp.dot(normed[span, :], wq[s, part], preferred_element_type=jnp.float32).astype(jnp.bfloat16)

    def swap(s, ref, name):
        push(ref.at[s, 0], ref.at[s, 1], arrival((name, s)), sibling)

    def block_of(n):
        return slice(n * rows, (n + 1) * rows)

    def seen_of(n):
        return [(0, n), (0, n ^ 1), (0, n ^ 2), (1, n)]

    def flag(n, side, other):
        of = 4 * (1 - half if side else half)
        return mask[zh, 4 * half + n, of + other] > 0

    def score(s, n):
        for hd in range(2):
            cols = slice(hd * HD, (hd + 1) * HD)
            query = q_ref[block_of(n), cols]
            scores, flags = [], []
            for side, other in seen_of(n):
                key = k_ref[s, side, block_of(other), cols]
                dots = lax.dot_general(query, key, (((1,), (1,)), ((), ())), preferred_element_type=jnp.float32)
                flags.append(flag(n, side, other))
                scores.append(jnp.where(flags[-1], dots * (1.0 / HD**0.5), NEG))
            top = jnp.max(functools.reduce(jnp.maximum, scores), axis=-1, keepdims=True)
            expos = [jnp.where(f, jnp.exp(v - top), 0.0) for f, v in zip(flags, scores)]
            total = jnp.sum(functools.reduce(jnp.add, expos), axis=-1, keepdims=True)
            for i, e in enumerate(expos):
                e_ref[n, hd, :, i * HD : (i + 1) * HD] = e.astype(jnp.bfloat16)
            t_ref[n, hd] = jnp.broadcast_to(total, (rows, HD))

    def mix(s, n):
        for hd in range(2):
            cols = slice(hd * HD, (hd + 1) * HD)
            summed = jnp.zeros((rows, HD), jnp.float32)
            for i, (side, other) in enumerate(seen_of(n)):
                summed = summed + jnp.dot(
                    e_ref[n, hd, :, i * HD : (i + 1) * HD], v_ref[s, side, block_of(other), cols],
                    preferred_element_type=jnp.float32,
                )
            attg[s, tile, block_of(n), cols] = (summed / t_ref[n, hd]).astype(jnp.bfloat16)

    def att_region(s, n):
        return lambda xx, yy, zz: attg.at[s, 2 * zz + xx, pl.ds(n * rows, rows), :]

    def attend(s, extra):
        arrive(k_ref.at[s, 1], arrival(("k", s)))
        for n in range(4):
            score(s, n)
        await_weights(s, VALUE)
        for g in range(2):
            span = slice(2 * g * rows, 2 * (g + 1) * rows)
            v_ref[s, 0, span, :] = project(s, VALUE, span)
        swap(s, v_ref, "v")
        arrive(v_ref.at[s, 1], arrival(("v", s)))
        spreads = []
        for n in range(4):
            mix(s, n)
            spreads.append(Spread(("a", s, n), "zx" if n % 2 else "xz", att_region(s, n)))
            spreads[-1].start()
        extra()
        await_projection(s)
        for n in range(4):
            spreads[n].stage(0)
        for n in range(4):
            spreads[n].stage(1)
            if n % 2:
                g = n // 2
                span = slice(2 * g * rows, 2 * (g + 1) * rows)
                lhs = jnp.concatenate([attg[s, i, span, :] for i in range(4)], axis=1)
                send_part[s, span, :] = jnp.dot(
                    lhs, wo[s, 1 - y], preferred_element_type=jnp.float32
                ).astype(jnp.bfloat16)
                push(
                    send_part.at[s, pl.ds(2 * g * rows, 2 * rows), :],
                    recv_part.at[s, pl.ds(2 * g * rows, 2 * rows), :],
                    arrival(("p", s, g)), partner["y"],
                )
                own_part[span, :] = jnp.dot(lhs, wo[s, y], preferred_element_type=jnp.float32)

    def total_of(s, g, before):
        span = slice(2 * g * rows, 2 * (g + 1) * rows)
        arrive(recv_part.at[s, pl.ds(2 * g * rows, 2 * rows), :], arrival(("p", s, g)))
        added = own_part[span, :] + recv_part[s, span, :].astype(jnp.float32)
        return (before(span).astype(jnp.float32) + added).astype(jnp.bfloat16)

    normalize(lambda n, span: xg[n, span, :], wide, 2, 0, 0, 4 * rows)
    every = slice(0, 4 * rows)
    await_weights(0, KEY)
    k_ref[0, 0] = project(0, KEY, every)
    swap(0, k_ref, "k")
    await_weights(0, QUERY)
    q_ref[...] = project(0, QUERY, every)
    attend(0, lambda: begin(weights[KEY], 1))
    begin(weights[QUERY], 1)
    rest_copy.wait()
    ms = [
        Spread(
            ("m", n), "zyx" if n % 2 else "zxy",
            lambda xx, yy, zz, n=n: midg.at[4 * yy + 2 * zz + xx, pl.ds(n * rows, rows), :],
        )
        for n in range(4)
    ]
    for g in range(2):
        midg[pair, 2 * g * rows : 2 * (g + 1) * rows, :] = total_of(0, g, lambda span: rest[span, :])
        for n in (2 * g, 2 * g + 1):
            ms[n].start()
    for m in ms:
        m.stage(0)
    begin(weights[VALUE] + wo_copies, 1)
    for m in ms:
        m.stage(1)
    for g in range(2):
        for n in (2 * g, 2 * g + 1):
            ms[n].stage(2)
        if g == 0:
            await_weights(1, KEY)
            await_weights(1, QUERY)
        span = slice(2 * g * rows, 2 * (g + 1) * rows)
        normalize(lambda n, at: midg[n, at, :], PAIR, 8, 1, 2 * g * rows, 2 * rows)
        k_ref[1, 0, span, :] = project(1, KEY, span)
        q_ref[span, :] = project(1, QUERY, span)
    swap(1, k_ref, "k")

    block = pl.ds(pl.multiple_of(tile * rows, rows), rows)
    outs = []
    for i in range(4):
        src, dst = midg.at[4 * y + i, block, :], out.at[zh, :, pl.ds(i * PAIR, PAIR)]
        outs.append(pltpu.make_async_copy(src, dst, loc.at[2 + i]))
        push(src, dst, arrival("mid"), dev(0, x, y, over), core == 1)

    @pl.when(core == 0)
    def _():
        for copy in outs:
            copy.start()

    attend(1, lambda: None)
    for g in range(2):
        fin[2 * g * rows : 2 * (g + 1) * rows, :] = total_of(1, g, lambda span: midg[pair, span, :])
        for n in (2 * g, 2 * g + 1):
            push(
                fin.at[pl.ds(n * rows, rows), :],
                out.at[zh, :, pl.ds(pl.multiple_of(tile * PAIR, PAIR), PAIR)],
                f_sem.at[zh], dev(1, n % 2, y, 2 * half + n // 2),
            )

    @pl.when(core == 0)
    def _():
        for copy in outs:
            copy.wait()
        arrive(out.at[1 - zh], arrival("mid"))

    @pl.when(core == 1)
    def _():
        for m in range(2):
            arrive(out.at[m], f_sem.at[m])

    for copy, when in sent:
        if when is None:
            copy.wait_send()
        else:
            pl.when(when)(copy.wait_send)


def local_cubes(feats, gain, w_qkv, w_out, block_mask):
    dma = pltpu.SemaphoreType.DMA
    bf, f32 = jnp.bfloat16, jnp.float32
    rows, wide = feats.shape[1], feats.shape[2]
    mine, whole = 4 * rows, 2 * wide
    vmem = pltpu.VMEM
    return pl.pallas_call(
        relay_kernel,
        out_shape=jax.ShapeDtypeStruct(feats.shape, bf),
        in_specs=[ANY] * 4 + [pl.BlockSpec(memory_space=pltpu.SMEM)],
        out_specs=ANY,
        scratch_shapes=[
            vmem((2, mine, wide), bf), vmem((mine, whole), bf), vmem((2, 1, whole), f32),
            vmem((2, 3, whole, PAIR), bf), vmem((2, 2, wide, PAIR), bf),
            vmem((mine, PAIR), bf), vmem((2, 2, mine, PAIR), bf), vmem((2, 2, mine, PAIR), bf),
            vmem((4, 2, rows, 4 * HD), bf), vmem((4, 2, rows, HD), f32),
            vmem((2, 4, mine, PAIR), bf), vmem((mine, PAIR), f32),
            vmem((2, mine, PAIR), bf), vmem((2, mine, PAIR), bf),
            vmem((mine, PAIR), bf), vmem((8, mine, PAIR), bf), vmem((mine, PAIR), bf),
            dma((140,)), dma((100,)), dma((2, 3)), dma((2, 2)), dma((2,)), dma((6,)),
        ],
        compiler_params=pltpu.CompilerParams(
            collective_id=0, has_side_effects=True, vmem_limit_bytes=63 * 2**20
        ),
        name="relay",
    )(feats, gain, w_qkv, w_out, block_mask)[None]


def solution(mesh):
    cubes = (mesh.shape["pipe"], mesh.shape["node"], mesh.shape["head"]) == (2, 8, 2)
    return jax.shard_map(
        local_cubes if cubes else local_any,
        mesh=mesh,
        in_specs=(
            P(None, "node", "head"),
            P("pipe", None),
            P("pipe", None, "node", "head"),
            P("pipe", "head", "node"),
            P(),
        ),
        out_specs=P("pipe", None, "node", "head"),
        check_vma=False,
    )
```

```python
import functools
import jax
import jax.numpy as jnp
from jax import lax
from jax.experimental import pallas as pl
from jax.experimental.pallas import tpu as pltpu
from jax.sharding import PartitionSpec as P

HD = 128
MICRO = 2


EPS = 1e-06
NEG = -1e30


def from_partner(block, axis, apart):
    count = lax.axis_size(axis)
    route = []
    for low in range(count):
        high = low | 1 << apart
        if high != low and high < count:
            route += [(low, high), (high, low)]
    return lax.ppermute(block, axis, route)


def from_behind(value, axis, steps):
    count = lax.axis_size(axis)
    first, last = (max(0, -steps), min(count, count - steps))
    return lax.ppermute(value, axis, [(source, source + steps) for source in range(first, last)])


def partial_attend(query, key, value, keep):
    rows = query.shape[0]
    groups = query.shape[1] // HD
    q_heads = query.reshape(rows, groups, HD)
    k_heads = key.reshape(key.shape[0], groups, HD)
    v_heads = value.reshape(value.shape[0], groups, HD)
    scores = jnp.einsum("qhd,khd->hqk", q_heads, k_heads, preferred_element_type=jnp.float32) * (
        1.0 / HD**0.5
    )
    scores = jnp.where(keep[None, None, :], scores, NEG)
    top = jnp.max(scores, axis=-1)
    expo = jnp.where(keep[None, None, :], jnp.exp(scores - top[..., None]), 0.0)
    total = jnp.sum(expo, axis=-1)
    summed = jnp.einsum(
        "hqk,khd->hqd", expo.astype(jnp.bfloat16), v_heads, preferred_element_type=jnp.float32
    )
    return (summed, top, total)


def finish(summed, total):
    out = summed / total[..., None]
    rows = out.shape[1]
    return jnp.transpose(out, (1, 0, 2)).reshape(rows, -1).astype(jnp.bfloat16)


def local_any(feats, gain, w_qkv, w_out, block_mask):
    segment = lax.axis_index("pipe")
    me = lax.axis_index("node")
    width = lax.axis_size("node").bit_length() - 1
    bit_list = [width - 1, width // 2, 0]
    qkv_whole, out_whole = (
        lax.all_gather(w_qkv, "node", axis=2, tiled=True),
        lax.all_gather(w_out, "node", axis=2, tiled=True),
    )
    w_query = qkv_whole[0, 0]
    w_key = qkv_whole[0, 1]
    w_value = qkv_whole[0, 2]
    w_proj = out_whole[0]
    gain_row = gain[0]
    rows = feats.shape[1]
    carried = jnp.zeros_like(feats[0])
    results = []
    for tick in range(MICRO + 1):
        micro = jnp.clip(tick - segment, 0, MICRO - 1)
        fresh = feats[min(tick, MICRO - 1)]
        inputs = jnp.where(segment == 0, fresh, carried)
        whole = lax.all_gather(inputs, "head", axis=1, tiled=True)
        xf = whole.astype(jnp.float32)
        inv = lax.rsqrt(jnp.mean(xf * xf, axis=-1, keepdims=True) + EPS)
        normed = (xf * inv * gain_row).astype(jnp.bfloat16)
        query = jnp.dot(normed, w_query, preferred_element_type=jnp.float32).astype(jnp.bfloat16)
        key = jnp.dot(normed, w_key, preferred_element_type=jnp.float32).astype(jnp.bfloat16)
        value = jnp.dot(normed, w_value, preferred_element_type=jnp.float32).astype(jnp.bfloat16)
        mask_rows = lax.dynamic_index_in_dim(block_mask, micro, 0, keepdims=False)
        own_flag = mask_rows[me, me] > 0
        key_list = [key]
        value_list = [value]
        flag_list = [own_flag]
        for bit in bit_list:
            far_key, far_value = from_partner((key, value), "node", bit)
            key_list.append(far_key)
            value_list.append(far_value)
            flag_list.append(mask_rows[me, jnp.bitwise_xor(me, 1 << bit)] > 0)
        keep = jnp.repeat(jnp.stack(flag_list), rows)
        summed, top, total = partial_attend(
            query, jnp.concatenate(key_list, 0), jnp.concatenate(value_list, 0), keep
        )
        attended = finish(summed, total)
        terms = jnp.dot(attended, w_proj, preferred_element_type=jnp.float32)
        reduced = lax.psum_scatter(
            terms.astype(jnp.bfloat16), "head", scatter_dimension=1, tiled=True
        ).astype(jnp.float32)
        output = (inputs.astype(jnp.float32) + reduced).astype(jnp.bfloat16)
        results.append(output)
        if tick < MICRO:
            carried = from_behind(output, "pipe", 1)
    first = jnp.where(segment == 0, results[0], results[1])
    second = jnp.where(segment == 0, results[1], results[2])
    return jnp.stack([first, second])[None]


MESH_ID = pl.DeviceIdType.MESH
ANY = pl.BlockSpec(memory_space=pl.ANY)
PAIR = 2 * HD
KEY, QUERY, VALUE = 1, 0, 2


def place():
    core, node, y = lax.axis_index("pipe"), lax.axis_index("node"), lax.axis_index("head")
    return core, lax.rem(node, 2), y, lax.div(node, 2)


def dev(core, x, y, z):
    return (core, z * 2 + x, y)


def z_apart(z, d):
    if d == 0:
        return z
    if d == 1:
        return z + 1 - 2 * lax.rem(z, 2)
    if d == 2:
        return z + 2 - 4 * lax.div(z, 2)
    return 3 - z


def remote(src, dst, send, recv, target):
    return pltpu.make_async_remote_copy(
        src_ref=src, dst_ref=dst, send_sem=send, recv_sem=recv, device_id=target, device_id_type=MESH_ID
    )


def greet(peers):
    barrier = pltpu.get_barrier_semaphore()
    for peer in peers:
        pl.semaphore_signal(barrier, inc=1, device_id=peer, device_id_type=MESH_ID)
    pl.semaphore_wait(barrier, len(peers))


def relay_kernel(
    feats, gain, w_qkv, w_out, mask, out,
    xg, normed, gains, wq, wo, q_ref, k_ref, v_ref, e_ref, t_ref, attg, own_part, send_part, recv_part,
    rest, midg, fin, snd, rcv, w_sem, o_sem, f_sem, loc,
):
    core, x, y, z = place()
    zh, zl = lax.div(z, 2), lax.rem(z, 2)
    half = core + zh - 2 * core * zh
    rows, wide = feats.shape[1], feats.shape[2]
    depth = w_qkv.shape[2]
    tile = 2 * zl + x
    pair = 4 * y + tile
    sibling, over = dev(1 - core, x, y, z), z_apart(z, 2)
    partner = {"x": dev(core, 1 - x, y, z), "y": dev(core, x, 1 - y, z), "z": dev(core, x, y, z_apart(z, 1))}
    greet(
        [
            dev(cc, xx, y, z_apart(z, d))
            for d in range(4)
            for xx in (x, 1 - x)
            for cc in (core, 1 - core)
        ][1:]
        + [partner["y"]]
    )
    names, sent, local = {}, [], []

    def arrival(key):
        return rcv.at[names.setdefault(key, len(names))]

    def make(src, dst, sem, target):
        copy = remote(src, dst, snd.at[len(sent)], sem, target)
        sent.append((copy, None))
        return copy

    def push(src, dst, sem, target, when=None):
        copy = remote(src, dst, snd.at[len(sent)], sem, target)
        sent.append((copy, when))
        if when is None:
            copy.start()
        else:
            pl.when(when)(copy.start)

    def arrive(dst, sem):
        remote(dst, dst, snd.at[0], sem, sibling).wait_recv()

    def keep(src, dst, sem):
        copy = pltpu.make_async_copy(src, dst, sem)
        copy.start()
        local.append(copy)

    class Spread:
        def __init__(self, tag, order, region):
            self.tag, self.order, self.region = tag, order, region

        def at(self, off):
            return self.region(
                1 - x if "x" in off else x, 1 - y if "y" in off else y, 1 - zl if "z" in off else zl
            )

        def key(self, off):
            return arrival((self.tag, "".join(sorted(off))))

        def pass_on(self, off, dims):
            spot = self.at(off)
            for d in dims:
                push(spot, spot, self.key(off + d), partner[d])

        def start(self):
            self.pass_on("", self.order)

        def take(self, off):
            arrive(self.at(off), self.key(off))
            last = max(self.order.index(d) for d in off)
            self.pass_on(off, self.order[last + 1 :])

        def stage(self, i):
            d = self.order[i]
            for n in range(1 << i):
                self.take("".join(self.order[b] for b in range(i) if n >> b & 1) + d)

    def weight_copies(part):
        copies = []
        to = wq.at[core, part, pl.ds(pl.multiple_of((2 * z + x) * depth, depth), depth), :]
        for d in (2, 3, 1, 0):
            for xx in (1 - x, x):
                zz = z_apart(z, d)
                spot = pl.multiple_of((2 * lax.rem(zz, 2) + xx) * PAIR, PAIR)
                src = w_qkv.at[0, part, :, pl.ds(spot, PAIR)]
                if d == 0 and xx is x:
                    copies.append(pltpu.make_async_copy(src, to, w_sem.at[core, part, zh]))
                else:
                    copies.append(make(src, to, w_sem.at[core, part, zh], dev(core, xx, y, zz)))
        return copies[:4], copies[4:]

    weights = {part: weight_copies(part) for part in (KEY, QUERY, VALUE)}
    own_wo = wo.at[core, zh]
    wo_copies = [
        make(w_out.at[0], own_wo, o_sem.at[core, zh], dev(core, x, y, over)),
        make(w_out.at[0], own_wo, o_sem.at[core, zh], sibling),
        pltpu.make_async_copy(w_out.at[0], own_wo, o_sem.at[core, zh]),
    ]

    def begin(copies, section):
        @pl.when(core == section)
        def _():
            for copy in copies:
                copy.start()

    def await_weights(s, part):
        for b in (zh, 1 - zh):
            got = wq.at[s, part, pl.ds(pl.multiple_of(b * 4 * depth, depth), 4 * depth), :]
            arrive(got, w_sem.at[s, part, b])
            push(got, got, w_sem.at[s, part, b], sibling, core == s)

    later = (
        weights[KEY][0] + weights[QUERY][0] + weights[KEY][1] + weights[VALUE][0] + weights[QUERY][1]
        + weights[VALUE][1] + wo_copies
    )

    def drip(count):
        begin(later[:count], 1)
        del later[:count]

    def await_projection(s):
        arrive(wo.at[s, zh], o_sem.at[s, zh])
        got = wo.at[s, 1 - zh]
        arrive(got, o_sem.at[s, 1 - zh])
        push(got, got, o_sem.at[s, 1 - zh], sibling, core == s)

    own_spot = xg.at[y, pl.ds(pl.multiple_of(tile * rows, rows), rows), :]
    own_key = arrival("own")
    cross = make(feats.at[1 - zh], own_spot, own_key, dev(core, x, y, over))
    sent.pop()
    sent.append((cross, core == 1))
    pl.when(core == 1)(cross.start)
    pl.when(core == 0)(pltpu.make_async_copy(feats.at[zh], own_spot, own_key).start)
    push(gain, gains.at[core], arrival("gain"), sibling)
    keep(gain, gains.at[core], loc.at[0])
    begin(weights[KEY][0], 0)
    arrive(own_spot, own_key)
    cut = rows // 2
    fs = [
        Spread(
            ("f", p), "zxy",
            lambda xx, yy, zz, p=p: xg.at[yy, pl.ds(pl.multiple_of((2 * zz + xx) * rows + p * cut, cut), cut), :],
        )
        for p in range(2)
    ]
    for f in fs:
        f.start()
    begin(weights[QUERY][0] + weights[KEY][1], 0)
    for f in fs:
        f.stage(0)
    begin(weights[VALUE][0] + weights[QUERY][1], 0)
    for f in fs:
        f.stage(1)
    begin(weights[VALUE][1] + wo_copies, 0)
    for f in fs:
        f.stage(2)
    arrive(gains.at[1 - core], arrival("gain"))
    local[0].wait()
    rest_copy = pltpu.make_async_copy(
        xg.at[y, :, pl.ds(pl.multiple_of(tile * PAIR, PAIR), PAIR)], rest, loc.at[1]
    )
    rest_copy.start()

    chunk = 16

    def normalize(load, width, count, s, first, length):
        def body(i, carry):
            span = pl.ds(pl.multiple_of(first + i * chunk, chunk), chunk)
            xs = [load(n, span).astype(jnp.float32) for n in range(count)]
            squares = functools.reduce(jnp.add, [jnp.sum(v * v, axis=-1, keepdims=True) for v in xs])
            inv = lax.rsqrt(squares * (1.0 / (width * count)) + EPS)
            for n, v in enumerate(xs):
                cols = slice(n * width, (n + 1) * width)
                normed[span, cols] = (v * inv * gains[s, :, cols]).astype(jnp.bfloat16)
            return carry

        lax.fori_loop(0, length // chunk, body, 0, unroll=2)

    def project(s, part, span):
        return jnp.dot(normed[span, :], wq[s, part], preferred_element_type=jnp.float32).astype(jnp.bfloat16)

    def swap(s, ref, name):
        push(ref.at[s, 0], ref.at[s, 1], arrival((name, s)), sibling)

    def block_of(n):
        return slice(n * rows, (n + 1) * rows)

    def seen_of(n):
        return [(0, n), (0, n ^ 1), (0, n ^ 2), (1, n)]

    def flag(n, side, other):
        of = 4 * (1 - half if side else half)
        return mask[zh, 4 * half + n, of + other] > 0

    def score(s, n):
        for hd in range(2):
            cols = slice(hd * HD, (hd + 1) * HD)
            query = q_ref[block_of(n), cols]
            scores, flags = [], []
            for side, other in seen_of(n):
                key = k_ref[s, side, block_of(other), cols]
                dots = lax.dot_general(query, key, (((1,), (1,)), ((), ())), preferred_element_type=jnp.float32)
                flags.append(flag(n, side, other))
                scores.append(jnp.where(flags[-1], dots * (1.0 / HD**0.5), NEG))
            top = jnp.max(functools.reduce(jnp.maximum, scores), axis=-1, keepdims=True)
            expos = [jnp.where(f, jnp.exp(v - top), 0.0) for f, v in zip(flags, scores)]
            total = jnp.sum(functools.reduce(jnp.add, expos), axis=-1, keepdims=True)
            for i, e in enumerate(expos):
                e_ref[n, hd, :, i * HD : (i + 1) * HD] = e.astype(jnp.bfloat16)
            t_ref[n, hd] = jnp.broadcast_to(total, (rows, HD))

    def mix(s, n):
        for hd in range(2):
            cols = slice(hd * HD, (hd + 1) * HD)
            summed = jnp.zeros((rows, HD), jnp.float32)
            for i, (side, other) in enumerate(seen_of(n)):
                summed = summed + jnp.dot(
                    e_ref[n, hd, :, i * HD : (i + 1) * HD], v_ref[s, side, block_of(other), cols],
                    preferred_element_type=jnp.float32,
                )
            attg[s, tile, block_of(n), cols] = (summed / t_ref[n, hd]).astype(jnp.bfloat16)

    def att_region(s, n):
        return lambda xx, yy, zz: attg.at[s, 2 * zz + xx, pl.ds(n * rows, rows), :]

    def strip(n):
        return pl.ds(n * rows, rows)

    def values(s):
        await_weights(s, VALUE)
        v_ref[s, 0] = project(s, VALUE, slice(0, 4 * rows))
        swap(s, v_ref, "v")

    def total_of(s, n, before):
        arrive(recv_part.at[s, strip(n), :], arrival(("p", s, n)))
        added = own_part[block_of(n), :] + recv_part[s, block_of(n), :].astype(jnp.float32)
        return (before[block_of(n), :].astype(jnp.float32) + added).astype(jnp.bfloat16)

    def attend(s, combine):
        if s == 1:
            values(s)
        arrive(k_ref.at[s, 1], arrival(("k", s)))
        for n in range(4):
            score(s, n)
        if s == 0:
            values(s)
        arrive(v_ref.at[s, 1], arrival(("v", s)))
        spreads = []
        for n in range(4):
            mix(s, n)
            spreads.append(Spread(("a", s, n), "zx" if n % 2 else "xz", att_region(s, n)))
            spreads[-1].start()
        drip(2)
        await_projection(s)
        for n in range(4):
            spreads[n].stage(0)
            drip(1)
        for n in range(4):
            spreads[n].stage(1)
            span = block_of(n)
            lhs = jnp.concatenate([attg[s, i, span, :] for i in range(4)], axis=1)
            send_part[s, span, :] = jnp.dot(lhs, wo[s, 1 - y], preferred_element_type=jnp.float32).astype(jnp.bfloat16)
            push(
                send_part.at[s, strip(n), :], recv_part.at[s, strip(n), :], arrival(("p", s, n)), partner["y"]
            )
            own_part[span, :] = jnp.dot(lhs, wo[s, y], preferred_element_type=jnp.float32)
            drip(1)
            if n:
                combine(n - 1)
        combine(3)

    normalize(lambda n, span: xg[n, span, :], wide, 2, 0, 0, 4 * rows)
    every = slice(0, 4 * rows)
    await_weights(0, KEY)
    k_ref[0, 0] = project(0, KEY, every)
    swap(0, k_ref, "k")
    await_weights(0, QUERY)
    q_ref[...] = project(0, QUERY, every)
    rest_copy.wait()
    ms = [
        Spread(
            ("m", n), "zyx" if n == 1 else "zxy",
            lambda xx, yy, zz, n=n: midg.at[4 * yy + 2 * zz + xx, strip(n), :],
        )
        for n in range(4)
    ]

    def middle(n):
        midg[pair, block_of(n), :] = total_of(0, n, rest)
        ms[n].start()
        drip(1)

    attend(0, middle)
    for m in ms:
        m.stage(0)
        drip(1)
    for m in ms:
        m.stage(1)
        drip(2)
    drip(len(later))
    await_weights(1, KEY)
    await_weights(1, QUERY)
    for n in range(4):
        ms[n].stage(2)
        normalize(lambda i, at: midg[i, at, :], PAIR, 8, 1, n * rows, rows)
        k_ref[1, 0, block_of(n), :] = project(1, KEY, block_of(n))
        q_ref[block_of(n), :] = project(1, QUERY, block_of(n))
    swap(1, k_ref, "k")

    block = pl.ds(pl.multiple_of(tile * rows, rows), rows)
    outs = []
    for i in range(4):
        src, dst = midg.at[4 * y + i, block, :], out.at[zh, :, pl.ds(i * PAIR, PAIR)]
        outs.append(pltpu.make_async_copy(src, dst, loc.at[2 + i]))
        push(src, dst, arrival("mid"), dev(0, x, y, over), core == 1)

    @pl.when(core == 0)
    def _():
        for copy in outs:
            copy.start()

    def last(n):
        fin[block_of(n), :] = total_of(1, n, midg.at[pair])
        push(
            fin.at[strip(n), :], out.at[zh, :, pl.ds(pl.multiple_of(tile * PAIR, PAIR), PAIR)],
            f_sem.at[zh], dev(1, n % 2, y, 2 * half + n // 2),
        )

    attend(1, last)

    @pl.when(core == 0)
    def _():
        for copy in outs:
            copy.wait()
        arrive(out.at[1 - zh], arrival("mid"))

    @pl.when(core == 1)
    def _():
        for m in range(2):
            arrive(out.at[m], f_sem.at[m])

    for copy, when in sent:
        if when is None:
            copy.wait_send()
        else:
            pl.when(when)(copy.wait_send)


def local_cubes(feats, gain, w_qkv, w_out, block_mask):
    dma = pltpu.SemaphoreType.DMA
    bf, f32 = jnp.bfloat16, jnp.float32
    rows, wide = feats.shape[1], feats.shape[2]
    mine, whole = 4 * rows, 2 * wide
    vmem = pltpu.VMEM
    return pl.pallas_call(
        relay_kernel,
        out_shape=jax.ShapeDtypeStruct(feats.shape, bf),
        in_specs=[ANY] * 4 + [pl.BlockSpec(memory_space=pltpu.SMEM)],
        out_specs=ANY,
        scratch_shapes=[
            vmem((2, mine, wide), bf), vmem((mine, whole), bf), vmem((2, 1, whole), f32),
            vmem((2, 3, whole, PAIR), bf), vmem((2, 2, wide, PAIR), bf),
            vmem((mine, PAIR), bf), vmem((2, 2, mine, PAIR), bf), vmem((2, 2, mine, PAIR), bf),
            vmem((4, 2, rows, 4 * HD), bf), vmem((4, 2, rows, HD), f32),
            vmem((2, 4, mine, PAIR), bf), vmem((mine, PAIR), f32),
            vmem((2, mine, PAIR), bf), vmem((2, mine, PAIR), bf),
            vmem((mine, PAIR), bf), vmem((8, mine, PAIR), bf), vmem((mine, PAIR), bf),
            dma((160,)), dma((110,)), dma((2, 3, 2)), dma((2, 2)), dma((2,)), dma((6,)),
        ],
        compiler_params=pltpu.CompilerParams(
            collective_id=0, has_side_effects=True, vmem_limit_bytes=63 * 2**20
        ),
        name="relay",
    )(feats, gain, w_qkv, w_out, block_mask)[None]


def solution(mesh):
    cubes = (mesh.shape["pipe"], mesh.shape["node"], mesh.shape["head"]) == (2, 8, 2)
    return jax.shard_map(
        local_cubes if cubes else local_any,
        mesh=mesh,
        in_specs=(
            P(None, "node", "head"),
            P("pipe", None),
            P("pipe", None, "node", "head"),
            P("pipe", "head", "node"),
            P(),
        ),
        out_specs=P("pipe", None, "node", "head"),
        check_vma=False,
    )
```

```python
import functools
import jax
import jax.numpy as jnp
from jax import lax
from jax.experimental import pallas as pl
from jax.experimental.pallas import tpu as pltpu
from jax.sharding import PartitionSpec as P

HD = 128
MICRO = 2


EPS = 1e-06
NEG = -1e30


def from_partner(block, axis, apart):
    count = lax.axis_size(axis)
    route = []
    for low in range(count):
        high = low | 1 << apart
        if high != low and high < count:
            route += [(low, high), (high, low)]
    return lax.ppermute(block, axis, route)


def from_behind(value, axis, steps):
    count = lax.axis_size(axis)
    first, last = (max(0, -steps), min(count, count - steps))
    return lax.ppermute(value, axis, [(source, source + steps) for source in range(first, last)])


def partial_attend(query, key, value, keep):
    rows = query.shape[0]
    groups = query.shape[1] // HD
    q_heads = query.reshape(rows, groups, HD)
    k_heads = key.reshape(key.shape[0], groups, HD)
    v_heads = value.reshape(value.shape[0], groups, HD)
    scores = jnp.einsum("qhd,khd->hqk", q_heads, k_heads, preferred_element_type=jnp.float32) * (
        1.0 / HD**0.5
    )
    scores = jnp.where(keep[None, None, :], scores, NEG)
    top = jnp.max(scores, axis=-1)
    expo = jnp.where(keep[None, None, :], jnp.exp(scores - top[..., None]), 0.0)
    total = jnp.sum(expo, axis=-1)
    summed = jnp.einsum(
        "hqk,khd->hqd", expo.astype(jnp.bfloat16), v_heads, preferred_element_type=jnp.float32
    )
    return (summed, top, total)


def finish(summed, total):
    out = summed / total[..., None]
    rows = out.shape[1]
    return jnp.transpose(out, (1, 0, 2)).reshape(rows, -1).astype(jnp.bfloat16)


def local_any(feats, gain, w_qkv, w_out, block_mask):
    segment = lax.axis_index("pipe")
    me = lax.axis_index("node")
    width = lax.axis_size("node").bit_length() - 1
    bit_list = [width - 1, width // 2, 0]
    qkv_whole, out_whole = (
        lax.all_gather(w_qkv, "node", axis=2, tiled=True),
        lax.all_gather(w_out, "node", axis=2, tiled=True),
    )
    w_query = qkv_whole[0, 0]
    w_key = qkv_whole[0, 1]
    w_value = qkv_whole[0, 2]
    w_proj = out_whole[0]
    gain_row = gain[0]
    rows = feats.shape[1]
    carried = jnp.zeros_like(feats[0])
    results = []
    for tick in range(MICRO + 1):
        micro = jnp.clip(tick - segment, 0, MICRO - 1)
        fresh = feats[min(tick, MICRO - 1)]
        inputs = jnp.where(segment == 0, fresh, carried)
        whole = lax.all_gather(inputs, "head", axis=1, tiled=True)
        xf = whole.astype(jnp.float32)
        inv = lax.rsqrt(jnp.mean(xf * xf, axis=-1, keepdims=True) + EPS)
        normed = (xf * inv * gain_row).astype(jnp.bfloat16)
        query = jnp.dot(normed, w_query, preferred_element_type=jnp.float32).astype(jnp.bfloat16)
        key = jnp.dot(normed, w_key, preferred_element_type=jnp.float32).astype(jnp.bfloat16)
        value = jnp.dot(normed, w_value, preferred_element_type=jnp.float32).astype(jnp.bfloat16)
        mask_rows = lax.dynamic_index_in_dim(block_mask, micro, 0, keepdims=False)
        own_flag = mask_rows[me, me] > 0
        key_list = [key]
        value_list = [value]
        flag_list = [own_flag]
        for bit in bit_list:
            far_key, far_value = from_partner((key, value), "node", bit)
            key_list.append(far_key)
            value_list.append(far_value)
            flag_list.append(mask_rows[me, jnp.bitwise_xor(me, 1 << bit)] > 0)
        keep = jnp.repeat(jnp.stack(flag_list), rows)
        summed, top, total = partial_attend(
            query, jnp.concatenate(key_list, 0), jnp.concatenate(value_list, 0), keep
        )
        attended = finish(summed, total)
        terms = jnp.dot(attended, w_proj, preferred_element_type=jnp.float32)
        reduced = lax.psum_scatter(
            terms.astype(jnp.bfloat16), "head", scatter_dimension=1, tiled=True
        ).astype(jnp.float32)
        output = (inputs.astype(jnp.float32) + reduced).astype(jnp.bfloat16)
        results.append(output)
        if tick < MICRO:
            carried = from_behind(output, "pipe", 1)
    first = jnp.where(segment == 0, results[0], results[1])
    second = jnp.where(segment == 0, results[1], results[2])
    return jnp.stack([first, second])[None]


MESH_ID = pl.DeviceIdType.MESH
ANY = pl.BlockSpec(memory_space=pl.ANY)
PAIR = 2 * HD
KEY, QUERY, VALUE = 1, 0, 2


def place():
    core, node, y = lax.axis_index("pipe"), lax.axis_index("node"), lax.axis_index("head")
    return core, lax.rem(node, 2), y, lax.div(node, 2)


def dev(core, x, y, z):
    return (core, z * 2 + x, y)


def z_apart(z, d):
    if d == 0:
        return z
    if d == 1:
        return z + 1 - 2 * lax.rem(z, 2)
    if d == 2:
        return z + 2 - 4 * lax.div(z, 2)
    return 3 - z


def remote(src, dst, send, recv, target):
    return pltpu.make_async_remote_copy(
        src_ref=src, dst_ref=dst, send_sem=send, recv_sem=recv, device_id=target, device_id_type=MESH_ID
    )


def greet(peers):
    barrier = pltpu.get_barrier_semaphore()
    for peer in peers:
        pl.semaphore_signal(barrier, inc=1, device_id=peer, device_id_type=MESH_ID)
    pl.semaphore_wait(barrier, len(peers))


def relay_kernel(
    feats, gain, w_qkv, w_out, mask, out,
    xg, normed, gains, wq, wo, q_ref, k_ref, v_ref, e_ref, t_ref, attg, own_part, send_part, recv_part,
    rest, midg, fin, snd, rcv, w_sem, o_sem, f_sem, loc,
):
    core, x, y, z = place()
    zh, zl = lax.div(z, 2), lax.rem(z, 2)
    half = core + zh - 2 * core * zh
    rows, wide = feats.shape[1], feats.shape[2]
    depth = w_qkv.shape[2]
    tile = 2 * zl + x
    pair = 4 * y + tile
    sibling, over = dev(1 - core, x, y, z), z_apart(z, 2)
    partner = {"x": dev(core, 1 - x, y, z), "y": dev(core, x, 1 - y, z), "z": dev(core, x, y, z_apart(z, 1))}
    greet(
        [
            dev(cc, xx, y, z_apart(z, d))
            for d in range(4)
            for xx in (x, 1 - x)
            for cc in (core, 1 - core)
        ][1:]
        + [partner["y"]]
    )
    names, sent, local = {}, [], []

    def arrival(key):
        return rcv.at[names.setdefault(key, len(names))]

    def make(src, dst, sem, target):
        copy = remote(src, dst, snd.at[len(sent)], sem, target)
        sent.append((copy, None))
        return copy

    def push(src, dst, sem, target, when=None):
        copy = remote(src, dst, snd.at[len(sent)], sem, target)
        sent.append((copy, when))
        if when is None:
            copy.start()
        else:
            pl.when(when)(copy.start)

    def arrive(dst, sem):
        remote(dst, dst, snd.at[0], sem, sibling).wait_recv()

    def keep(src, dst, sem):
        copy = pltpu.make_async_copy(src, dst, sem)
        copy.start()
        local.append(copy)

    class Spread:
        def __init__(self, tag, order, region):
            self.tag, self.order, self.region = tag, order, region

        def at(self, off):
            return self.region(
                1 - x if "x" in off else x, 1 - y if "y" in off else y, 1 - zl if "z" in off else zl
            )

        def key(self, off):
            return arrival((self.tag, "".join(sorted(off))))

        def pass_on(self, off, dims):
            spot = self.at(off)
            for d in dims:
                push(spot, spot, self.key(off + d), partner[d])

        def start(self):
            self.pass_on("", self.order)

        def take(self, off):
            arrive(self.at(off), self.key(off))
            last = max(self.order.index(d) for d in off)
            self.pass_on(off, self.order[last + 1 :])

        def stage(self, i):
            d = self.order[i]
            for n in range(1 << i):
                self.take("".join(self.order[b] for b in range(i) if n >> b & 1) + d)

    def weight_copies(part):
        copies = []
        to = wq.at[core, part, zh, pl.ds(pl.multiple_of(tile * depth, depth), depth), :]
        for d in (2, 3, 1, 0):
            for xx in (1 - x, x):
                zz = z_apart(z, d)
                spot = pl.multiple_of((2 * lax.rem(zz, 2) + xx) * PAIR, PAIR)
                src = w_qkv.at[0, part, :, pl.ds(spot, PAIR)]
                if d == 0 and xx is x:
                    copies.append(pltpu.make_async_copy(src, to, w_sem.at[core, part, zh]))
                else:
                    copies.append(make(src, to, w_sem.at[core, part, zh], dev(core, xx, y, zz)))
        return copies[:4], copies[4:]

    weights = {part: weight_copies(part) for part in (KEY, QUERY, VALUE)}
    own_wo = wo.at[core, zh]
    wo_copies = [
        make(w_out.at[0], own_wo, o_sem.at[core, zh], dev(core, x, y, over)),
        make(w_out.at[0], own_wo, o_sem.at[core, zh], sibling),
        pltpu.make_async_copy(w_out.at[0], own_wo, o_sem.at[core, zh]),
    ]

    def begin(copies, section):
        @pl.when(core == section)
        def _():
            for copy in copies:
                copy.start()

    def await_weights(s, part, b):
        got = wq.at[s, part, b]
        arrive(got, w_sem.at[s, part, b])
        push(got, got, w_sem.at[s, part, b], sibling, core == s)

    later = (
        weights[KEY][0] + weights[QUERY][0] + weights[KEY][1] + weights[QUERY][1] + weights[VALUE][0]
        + weights[VALUE][1] + wo_copies
    )

    def drip(count):
        begin(later[:count], 1)
        del later[:count]

    def await_projection(s):
        arrive(wo.at[s, zh], o_sem.at[s, zh])
        got = wo.at[s, 1 - zh]
        arrive(got, o_sem.at[s, 1 - zh])
        push(got, got, o_sem.at[s, 1 - zh], sibling, core == s)

    own_spot = xg.at[y, pl.ds(pl.multiple_of(tile * rows, rows), rows), :]
    own_key = arrival("own")
    cross = make(feats.at[1 - zh], own_spot, own_key, dev(core, x, y, over))
    sent.pop()
    sent.append((cross, core == 1))
    pl.when(core == 1)(cross.start)
    pl.when(core == 0)(pltpu.make_async_copy(feats.at[zh], own_spot, own_key).start)
    push(gain, gains.at[core], arrival("gain"), sibling)
    keep(gain, gains.at[core], loc.at[0])
    begin(weights[KEY][0], 0)
    arrive(own_spot, own_key)
    cut = rows // 2
    fs = [
        Spread(
            ("f", p), "zxy",
            lambda xx, yy, zz, p=p: xg.at[yy, pl.ds(pl.multiple_of((2 * zz + xx) * rows + p * cut, cut), cut), :],
        )
        for p in range(2)
    ]
    for f in fs:
        f.start()
    begin(weights[QUERY][0] + weights[KEY][1], 0)
    for f in fs:
        f.stage(0)
    begin(weights[VALUE][0] + weights[QUERY][1], 0)
    for f in fs:
        f.stage(1)
    begin(weights[VALUE][1] + wo_copies, 0)
    for f in fs:
        f.stage(2)
    arrive(gains.at[1 - core], arrival("gain"))
    local[0].wait()
    rest_copy = pltpu.make_async_copy(
        xg.at[y, :, pl.ds(pl.multiple_of(tile * PAIR, PAIR), PAIR)], rest, loc.at[1]
    )
    rest_copy.start()

    chunk = 16

    def normalize(load, width, count, s, first, length):
        def body(i, carry):
            span = pl.ds(pl.multiple_of(first + i * chunk, chunk), chunk)
            xs = [load(n, span).astype(jnp.float32) for n in range(count)]
            squares = functools.reduce(jnp.add, [jnp.sum(v * v, axis=-1, keepdims=True) for v in xs])
            inv = lax.rsqrt(squares * (1.0 / (width * count)) + EPS)
            for n, v in enumerate(xs):
                cols = slice(n * width, (n + 1) * width)
                b, at = divmod(n * width, wide)
                normed[b, span, at : at + width] = (v * inv * gains[s, :, cols]).astype(jnp.bfloat16)
            return carry

        lax.fori_loop(0, length // chunk, body, 0, unroll=2)

    def project(s, part, span, wait=True):
        total = None
        for b in (zh, 1 - zh):
            if wait:
                await_weights(s, part, b)
            term = jnp.dot(normed[b, span, :], wq[s, part, b], preferred_element_type=jnp.float32)
            total = term if total is None else total + term
        return total.astype(jnp.bfloat16)

    def swap(s, ref, name):
        push(ref.at[s, 0], ref.at[s, 1], arrival((name, s)), sibling)

    def block_of(n):
        return slice(n * rows, (n + 1) * rows)

    def seen_of(n):
        return [(0, n), (0, n ^ 1), (0, n ^ 2), (1, n)]

    def flag(n, side, other):
        of = 4 * (1 - half if side else half)
        return mask[zh, 4 * half + n, of + other] > 0

    def score(s, n):
        for hd in range(2):
            cols = slice(hd * HD, (hd + 1) * HD)
            query = q_ref[block_of(n), cols]
            scores, flags = [], []
            for side, other in seen_of(n):
                key = k_ref[s, side, block_of(other), cols]
                dots = lax.dot_general(query, key, (((1,), (1,)), ((), ())), preferred_element_type=jnp.float32)
                flags.append(flag(n, side, other))
                scores.append(jnp.where(flags[-1], dots * (1.0 / HD**0.5), NEG))
            top = jnp.max(functools.reduce(jnp.maximum, scores), axis=-1, keepdims=True)
            expos = [jnp.where(f, jnp.exp(v - top), 0.0) for f, v in zip(flags, scores)]
            total = jnp.sum(functools.reduce(jnp.add, expos), axis=-1, keepdims=True)
            for i, e in enumerate(expos):
                e_ref[n, hd, :, i * HD : (i + 1) * HD] = e.astype(jnp.bfloat16)
            t_ref[n, hd] = jnp.broadcast_to(total, (rows, HD))

    def mix(s, n):
        for hd in range(2):
            cols = slice(hd * HD, (hd + 1) * HD)
            summed = jnp.zeros((rows, HD), jnp.float32)
            for i, (side, other) in enumerate(seen_of(n)):
                summed = summed + jnp.dot(
                    e_ref[n, hd, :, i * HD : (i + 1) * HD], v_ref[s, side, block_of(other), cols],
                    preferred_element_type=jnp.float32,
                )
            attg[s, tile, block_of(n), cols] = (summed / t_ref[n, hd]).astype(jnp.bfloat16)

    def att_region(s, n):
        return lambda xx, yy, zz: attg.at[s, 2 * zz + xx, pl.ds(n * rows, rows), :]

    def strip(n):
        return pl.ds(n * rows, rows)

    def values(s):
        v_ref[s, 0] = project(s, VALUE, slice(0, 4 * rows))
        swap(s, v_ref, "v")

    def total_of(s, n, before):
        arrive(recv_part.at[s, strip(n), :], arrival(("p", s, n)))
        added = own_part[block_of(n), :] + recv_part[s, block_of(n), :].astype(jnp.float32)
        return (before[block_of(n), :].astype(jnp.float32) + added).astype(jnp.bfloat16)

    def attend(s, combine, between):
        if s == 1:
            values(s)
        arrive(k_ref.at[s, 1], arrival(("k", s)))
        for n in range(4):
            score(s, n)
        if s == 0:
            values(s)
        arrive(v_ref.at[s, 1], arrival(("v", s)))
        spreads = []
        for n in range(4):
            mix(s, n)
            spreads.append(Spread(("a", s, n), "zx" if n % 2 else "xz", att_region(s, n)))
            spreads[-1].start()
        drip(1)
        await_projection(s)
        for n in range(4):
            spreads[n].stage(0)
            drip(1)
        between()
        for n in range(4):
            spreads[n].stage(1)
            span = block_of(n)
            lhs = jnp.concatenate([attg[s, i, span, :] for i in range(4)], axis=1)
            send_part[s, span, :] = jnp.dot(lhs, wo[s, 1 - y], preferred_element_type=jnp.float32).astype(jnp.bfloat16)
            push(
                send_part.at[s, strip(n), :], recv_part.at[s, strip(n), :], arrival(("p", s, n)), partner["y"]
            )
            own_part[span, :] = jnp.dot(lhs, wo[s, y], preferred_element_type=jnp.float32)
            drip(1)
            if n:
                combine(n - 1)
        combine(3)

    normalize(lambda n, span: xg[n, span, :], wide, 2, 0, 0, 4 * rows)
    every = slice(0, 4 * rows)
    k_ref[0, 0] = project(0, KEY, every)
    swap(0, k_ref, "k")
    q_ref[...] = project(0, QUERY, every)
    rest_copy.wait()
    ms = [
        Spread(
            ("m", n), "zyx" if n == 1 else "zxy",
            lambda xx, yy, zz, n=n: midg.at[4 * yy + 2 * zz + xx, strip(n), :],
        )
        for n in range(4)
    ]

    def middle(n):
        midg[pair, block_of(n), :] = total_of(0, n, rest)
        ms[n].start()
        drip(2)

    attend(0, middle, lambda: None)
    for m in ms:
        m.stage(0)
        drip(1)
    for m in ms:
        m.stage(1)
        drip(2)
    drip(len(later))
    for part in (KEY, QUERY):
        for b in (zh, 1 - zh):
            await_weights(1, part, b)
    for n in range(4):
        ms[n].stage(2)
        normalize(lambda i, at: midg[i, at, :], PAIR, 8, 1, n * rows, rows)
        k_ref[1, 0, block_of(n), :] = project(1, KEY, block_of(n), False)
        q_ref[block_of(n), :] = project(1, QUERY, block_of(n), False)
    swap(1, k_ref, "k")

    block = pl.ds(pl.multiple_of(tile * rows, rows), rows)
    outs = []

    def first_output():
        for i in range(4):
            src, dst = midg.at[4 * y + i, block, :], out.at[zh, :, pl.ds(i * PAIR, PAIR)]
            outs.append(pltpu.make_async_copy(src, dst, loc.at[2 + i]))
            push(src, dst, arrival("mid"), dev(0, x, y, over), core == 1)

        @pl.when(core == 0)
        def _():
            for copy in outs:
                copy.start()

    def last(n):
        fin[block_of(n), :] = total_of(1, n, midg.at[pair])
        push(
            fin.at[strip(n), :], out.at[zh, :, pl.ds(pl.multiple_of(tile * PAIR, PAIR), PAIR)],
            f_sem.at[zh], dev(1, n % 2, y, 2 * half + n // 2),
        )

    attend(1, last, first_output)

    @pl.when(core == 0)
    def _():
        for copy in outs:
            copy.wait()
        arrive(out.at[1 - zh], arrival("mid"))

    @pl.when(core == 1)
    def _():
        for m in range(2):
            arrive(out.at[m], f_sem.at[m])

    for copy, when in sent:
        if when is None:
            copy.wait_send()
        else:
            pl.when(when)(copy.wait_send)


def local_cubes(feats, gain, w_qkv, w_out, block_mask):
    dma = pltpu.SemaphoreType.DMA
    bf, f32 = jnp.bfloat16, jnp.float32
    rows, wide = feats.shape[1], feats.shape[2]
    mine, whole = 4 * rows, 2 * wide
    vmem = pltpu.VMEM
    return pl.pallas_call(
        relay_kernel,
        out_shape=jax.ShapeDtypeStruct(feats.shape, bf),
        in_specs=[ANY] * 4 + [pl.BlockSpec(memory_space=pltpu.SMEM)],
        out_specs=ANY,
        scratch_shapes=[
            vmem((2, mine, wide), bf), vmem((2, mine, wide), bf), vmem((2, 1, whole), f32),
            vmem((2, 3, 2, wide, PAIR), bf), vmem((2, 2, wide, PAIR), bf),
            vmem((mine, PAIR), bf), vmem((2, 2, mine, PAIR), bf), vmem((2, 2, mine, PAIR), bf),
            vmem((4, 2, rows, 4 * HD), bf), vmem((4, 2, rows, HD), f32),
            vmem((2, 4, mine, PAIR), bf), vmem((mine, PAIR), f32),
            vmem((2, mine, PAIR), bf), vmem((2, mine, PAIR), bf),
            vmem((mine, PAIR), bf), vmem((8, mine, PAIR), bf), vmem((mine, PAIR), bf),
            dma((160,)), dma((110,)), dma((2, 3, 2)), dma((2, 2)), dma((2,)), dma((6,)),
        ],
        compiler_params=pltpu.CompilerParams(
            collective_id=0, has_side_effects=True, vmem_limit_bytes=63 * 2**20
        ),
        name="relay",
    )(feats, gain, w_qkv, w_out, block_mask)[None]


def solution(mesh):
    cubes = (mesh.shape["pipe"], mesh.shape["node"], mesh.shape["head"]) == (2, 8, 2)
    return jax.shard_map(
        local_cubes if cubes else local_any,
        mesh=mesh,
        in_specs=(
            P(None, "node", "head"),
            P("pipe", None),
            P("pipe", None, "node", "head"),
            P("pipe", "head", "node"),
            P(),
        ),
        out_specs=P("pipe", None, "node", "head"),
        check_vma=False,
    )
```

```python
import functools
import jax
import jax.numpy as jnp
from jax import lax
from jax.experimental import pallas as pl
from jax.experimental.pallas import tpu as pltpu
from jax.sharding import PartitionSpec as P

HD = 128
MICRO = 2


EPS = 1e-06
NEG = -1e30


def from_partner(block, axis, apart):
    count = lax.axis_size(axis)
    route = []
    for low in range(count):
        high = low | 1 << apart
        if high != low and high < count:
            route += [(low, high), (high, low)]
    return lax.ppermute(block, axis, route)


def from_behind(value, axis, steps):
    count = lax.axis_size(axis)
    first, last = (max(0, -steps), min(count, count - steps))
    return lax.ppermute(value, axis, [(source, source + steps) for source in range(first, last)])


def partial_attend(query, key, value, keep):
    rows = query.shape[0]
    groups = query.shape[1] // HD
    q_heads = query.reshape(rows, groups, HD)
    k_heads = key.reshape(key.shape[0], groups, HD)
    v_heads = value.reshape(value.shape[0], groups, HD)
    scores = jnp.einsum("qhd,khd->hqk", q_heads, k_heads, preferred_element_type=jnp.float32) * (
        1.0 / HD**0.5
    )
    scores = jnp.where(keep[None, None, :], scores, NEG)
    top = jnp.max(scores, axis=-1)
    expo = jnp.where(keep[None, None, :], jnp.exp(scores - top[..., None]), 0.0)
    total = jnp.sum(expo, axis=-1)
    summed = jnp.einsum(
        "hqk,khd->hqd", expo.astype(jnp.bfloat16), v_heads, preferred_element_type=jnp.float32
    )
    return (summed, top, total)


def finish(summed, total):
    out = summed / total[..., None]
    rows = out.shape[1]
    return jnp.transpose(out, (1, 0, 2)).reshape(rows, -1).astype(jnp.bfloat16)


def local_any(feats, gain, w_qkv, w_out, block_mask):
    segment = lax.axis_index("pipe")
    me = lax.axis_index("node")
    width = lax.axis_size("node").bit_length() - 1
    bit_list = [width - 1, width // 2, 0]
    qkv_whole, out_whole = (
        lax.all_gather(w_qkv, "node", axis=2, tiled=True),
        lax.all_gather(w_out, "node", axis=2, tiled=True),
    )
    w_query = qkv_whole[0, 0]
    w_key = qkv_whole[0, 1]
    w_value = qkv_whole[0, 2]
    w_proj = out_whole[0]
    gain_row = gain[0]
    rows = feats.shape[1]
    carried = jnp.zeros_like(feats[0])
    results = []
    for tick in range(MICRO + 1):
        micro = jnp.clip(tick - segment, 0, MICRO - 1)
        fresh = feats[min(tick, MICRO - 1)]
        inputs = jnp.where(segment == 0, fresh, carried)
        whole = lax.all_gather(inputs, "head", axis=1, tiled=True)
        xf = whole.astype(jnp.float32)
        inv = lax.rsqrt(jnp.mean(xf * xf, axis=-1, keepdims=True) + EPS)
        normed = (xf * inv * gain_row).astype(jnp.bfloat16)
        query = jnp.dot(normed, w_query, preferred_element_type=jnp.float32).astype(jnp.bfloat16)
        key = jnp.dot(normed, w_key, preferred_element_type=jnp.float32).astype(jnp.bfloat16)
        value = jnp.dot(normed, w_value, preferred_element_type=jnp.float32).astype(jnp.bfloat16)
        mask_rows = lax.dynamic_index_in_dim(block_mask, micro, 0, keepdims=False)
        own_flag = mask_rows[me, me] > 0
        key_list = [key]
        value_list = [value]
        flag_list = [own_flag]
        for bit in bit_list:
            far_key, far_value = from_partner((key, value), "node", bit)
            key_list.append(far_key)
            value_list.append(far_value)
            flag_list.append(mask_rows[me, jnp.bitwise_xor(me, 1 << bit)] > 0)
        keep = jnp.repeat(jnp.stack(flag_list), rows)
        summed, top, total = partial_attend(
            query, jnp.concatenate(key_list, 0), jnp.concatenate(value_list, 0), keep
        )
        attended = finish(summed, total)
        terms = jnp.dot(attended, w_proj, preferred_element_type=jnp.float32)
        reduced = lax.psum_scatter(
            terms.astype(jnp.bfloat16), "head", scatter_dimension=1, tiled=True
        ).astype(jnp.float32)
        output = (inputs.astype(jnp.float32) + reduced).astype(jnp.bfloat16)
        results.append(output)
        if tick < MICRO:
            carried = from_behind(output, "pipe", 1)
    first = jnp.where(segment == 0, results[0], results[1])
    second = jnp.where(segment == 0, results[1], results[2])
    return jnp.stack([first, second])[None]


MESH_ID = pl.DeviceIdType.MESH
ANY = pl.BlockSpec(memory_space=pl.ANY)
PAIR = 2 * HD
KEY, QUERY, VALUE = 1, 0, 2


def place():
    core, node, y = lax.axis_index("pipe"), lax.axis_index("node"), lax.axis_index("head")
    return core, lax.rem(node, 2), y, lax.div(node, 2)


def dev(core, x, y, z):
    return (core, z * 2 + x, y)


def z_apart(z, d):
    if d == 0:
        return z
    if d == 1:
        return z + 1 - 2 * lax.rem(z, 2)
    if d == 2:
        return z + 2 - 4 * lax.div(z, 2)
    return 3 - z


def remote(src, dst, send, recv, target):
    return pltpu.make_async_remote_copy(
        src_ref=src, dst_ref=dst, send_sem=send, recv_sem=recv, device_id=target, device_id_type=MESH_ID
    )


def greet(peers):
    barrier = pltpu.get_barrier_semaphore()
    for peer in peers:
        pl.semaphore_signal(barrier, inc=1, device_id=peer, device_id_type=MESH_ID)
    pl.semaphore_wait(barrier, len(peers))


def relay_kernel(
    feats, gain, w_qkv, w_out, mask, out,
    xg, normed, gains, wq, wo, q_ref, k_ref, v_ref, e_ref, t_ref, attg, own_part, send_part, recv_part,
    rest, midg, fin, snd, rcv, w_sem, o_sem, f_sem, loc,
):
    core, x, y, z = place()
    zh, zl = lax.div(z, 2), lax.rem(z, 2)
    half = core + zh - 2 * core * zh
    rows, wide = feats.shape[1], feats.shape[2]
    depth = w_qkv.shape[2]
    tile = 2 * zl + x
    pair = 4 * y + tile
    sibling, over = dev(1 - core, x, y, z), z_apart(z, 2)
    partner = {"x": dev(core, 1 - x, y, z), "y": dev(core, x, 1 - y, z), "z": dev(core, x, y, z_apart(z, 1))}
    greet(
        [
            dev(cc, xx, y, z_apart(z, d))
            for d in range(4)
            for xx in (x, 1 - x)
            for cc in (core, 1 - core)
        ][1:]
        + [partner["y"]]
    )
    names, sent, local = {}, [], []

    def arrival(key):
        return rcv.at[names.setdefault(key, len(names))]

    def make(src, dst, sem, target):
        copy = remote(src, dst, snd.at[len(sent)], sem, target)
        sent.append((copy, None))
        return copy

    def push(src, dst, sem, target, when=None):
        copy = remote(src, dst, snd.at[len(sent)], sem, target)
        sent.append((copy, when))
        if when is None:
            copy.start()
        else:
            pl.when(when)(copy.start)

    def arrive(dst, sem):
        remote(dst, dst, snd.at[0], sem, sibling).wait_recv()

    def keep(src, dst, sem):
        copy = pltpu.make_async_copy(src, dst, sem)
        copy.start()
        local.append(copy)

    class Spread:
        def __init__(self, tag, order, region):
            self.tag, self.order, self.region = tag, order, region

        def at(self, off):
            return self.region(
                1 - x if "x" in off else x, 1 - y if "y" in off else y, 1 - zl if "z" in off else zl
            )

        def key(self, off):
            return arrival((self.tag, "".join(sorted(off))))

        def pass_on(self, off, dims):
            spot = self.at(off)
            for d in dims:
                push(spot, spot, self.key(off + d), partner[d])

        def start(self):
            self.pass_on("", self.order)

        def take(self, off):
            arrive(self.at(off), self.key(off))
            last = max(self.order.index(d) for d in off)
            self.pass_on(off, self.order[last + 1 :])

        def stage(self, i):
            d = self.order[i]
            for n in range(1 << i):
                self.take("".join(self.order[b] for b in range(i) if n >> b & 1) + d)

    def weight_copies(part):
        copies = []
        to = wq.at[core, part, zh, pl.ds(pl.multiple_of(tile * depth, depth), depth), :]
        for d in (2, 3, 1, 0):
            for xx in (1 - x, x):
                zz = z_apart(z, d)
                spot = pl.multiple_of((2 * lax.rem(zz, 2) + xx) * PAIR, PAIR)
                src = w_qkv.at[0, part, :, pl.ds(spot, PAIR)]
                if d == 0 and xx is x:
                    copies.append(pltpu.make_async_copy(src, to, w_sem.at[core, part, zh]))
                else:
                    copies.append(make(src, to, w_sem.at[core, part, zh], dev(core, xx, y, zz)))
        return copies[:4], copies[4:]

    weights = {part: weight_copies(part) for part in (KEY, QUERY, VALUE)}
    own_wo = wo.at[core, zh]
    wo_copies = [
        make(w_out.at[0], own_wo, o_sem.at[core, zh], dev(core, x, y, over)),
        make(w_out.at[0], own_wo, o_sem.at[core, zh], sibling),
        pltpu.make_async_copy(w_out.at[0], own_wo, o_sem.at[core, zh]),
    ]

    def begin(copies, section):
        @pl.when(core == section)
        def _():
            for copy in copies:
                copy.start()

    def await_weights(s, part, b):
        got = wq.at[s, part, b]
        arrive(got, w_sem.at[s, part, b])
        push(got, got, w_sem.at[s, part, b], sibling, core == s)

    later = (
        weights[KEY][0] + weights[QUERY][0] + weights[KEY][1] + weights[QUERY][1] + weights[VALUE][0]
        + weights[VALUE][1] + wo_copies
    )

    def drip(count):
        begin(later[:count], 1)
        del later[:count]

    def await_projection(s):
        arrive(wo.at[s, zh], o_sem.at[s, zh])
        got = wo.at[s, 1 - zh]
        arrive(got, o_sem.at[s, 1 - zh])
        push(got, got, o_sem.at[s, 1 - zh], sibling, core == s)

    own_spot = xg.at[y, pl.ds(pl.multiple_of(tile * rows, rows), rows), :]
    own_key = arrival("own")
    cross = make(feats.at[1 - zh], own_spot, own_key, dev(core, x, y, over))
    sent.pop()
    sent.append((cross, core == 1))
    pl.when(core == 1)(cross.start)
    pl.when(core == 0)(pltpu.make_async_copy(feats.at[zh], own_spot, own_key).start)
    push(gain, gains.at[core], arrival("gain"), sibling)
    keep(gain, gains.at[core], loc.at[0])
    begin(weights[KEY][0], 0)
    arrive(own_spot, own_key)
    cut = rows // 2
    fs = [
        Spread(
            ("f", p), "zxy",
            lambda xx, yy, zz, p=p: xg.at[yy, pl.ds(pl.multiple_of((2 * zz + xx) * rows + p * cut, cut), cut), :],
        )
        for p in range(2)
    ]
    for f in fs:
        f.start()
    begin(weights[QUERY][0] + weights[KEY][1], 0)
    for f in fs:
        f.stage(0)
    begin(weights[VALUE][0] + weights[QUERY][1], 0)
    for f in fs:
        f.stage(1)
    begin(weights[VALUE][1] + wo_copies, 0)
    for f in fs:
        f.stage(2)
    arrive(gains.at[1 - core], arrival("gain"))
    local[0].wait()
    rest_copy = pltpu.make_async_copy(
        xg.at[y, :, pl.ds(pl.multiple_of(tile * PAIR, PAIR), PAIR)], rest, loc.at[1]
    )
    rest_copy.start()

    chunk = 16

    def normalize(load, width, count, s, first, length):
        def body(i, carry):
            span = pl.ds(pl.multiple_of(first + i * chunk, chunk), chunk)
            xs = [load(n, span).astype(jnp.float32) for n in range(count)]
            squares = functools.reduce(jnp.add, [jnp.sum(v * v, axis=-1, keepdims=True) for v in xs])
            inv = lax.rsqrt(squares * (1.0 / (width * count)) + EPS)
            for n, v in enumerate(xs):
                cols = slice(n * width, (n + 1) * width)
                b, at = divmod(n * width, wide)
                normed[b, span, at : at + width] = (v * inv * gains[s, :, cols]).astype(jnp.bfloat16)
            return carry

        lax.fori_loop(0, length // chunk, body, 0, unroll=2)

    def project(s, part, span, wait=True):
        total = None
        for b in (zh, 1 - zh):
            if wait:
                await_weights(s, part, b)
            term = jnp.dot(normed[b, span, :], wq[s, part, b], preferred_element_type=jnp.float32)
            total = term if total is None else total + term
        return total.astype(jnp.bfloat16)

    def swap(s, ref, name):
        push(ref.at[s, 0], ref.at[s, 1], arrival((name, s)), sibling)

    def block_of(n):
        return slice(n * rows, (n + 1) * rows)

    def seen_of(n):
        return [(0, n), (0, n ^ 1), (0, n ^ 2), (1, n)]

    def flag(n, side, other):
        of = 4 * (1 - half if side else half)
        return mask[zh, 4 * half + n, of + other] > 0

    def score(s, n):
        for hd in range(2):
            cols = slice(hd * HD, (hd + 1) * HD)
            query = q_ref[block_of(n), cols]
            scores, flags = [], []
            for side, other in seen_of(n):
                key = k_ref[s, side, block_of(other), cols]
                dots = lax.dot_general(query, key, (((1,), (1,)), ((), ())), preferred_element_type=jnp.float32)
                flags.append(flag(n, side, other))
                scores.append(jnp.where(flags[-1], dots * (1.0 / HD**0.5), NEG))
            top = jnp.max(functools.reduce(jnp.maximum, scores), axis=-1, keepdims=True)
            expos = [jnp.where(f, jnp.exp(v - top), 0.0) for f, v in zip(flags, scores)]
            total = jnp.sum(functools.reduce(jnp.add, expos), axis=-1, keepdims=True)
            for i, e in enumerate(expos):
                e_ref[n, hd, :, i * HD : (i + 1) * HD] = e.astype(jnp.bfloat16)
            t_ref[n, hd] = jnp.broadcast_to(total, (rows, HD))

    def mix(s, n):
        for hd in range(2):
            cols = slice(hd * HD, (hd + 1) * HD)
            summed = jnp.zeros((rows, HD), jnp.float32)
            for i, (side, other) in enumerate(seen_of(n)):
                summed = summed + jnp.dot(
                    e_ref[n, hd, :, i * HD : (i + 1) * HD], v_ref[s, side, block_of(other), cols],
                    preferred_element_type=jnp.float32,
                )
            attg[s, tile, block_of(n), cols] = (summed / t_ref[n, hd]).astype(jnp.bfloat16)

    def att_region(s, n):
        return lambda xx, yy, zz: attg.at[s, 2 * zz + xx, pl.ds(n * rows, rows), :]

    def strip(n):
        return pl.ds(n * rows, rows)

    def values(s):
        v_ref[s, 0] = project(s, VALUE, slice(0, 4 * rows))
        swap(s, v_ref, "v")

    def total_of(s, n, before):
        arrive(recv_part.at[s, strip(n), :], arrival(("p", s, n)))
        added = own_part[block_of(n), :] + recv_part[s, block_of(n), :].astype(jnp.float32)
        return (before[block_of(n), :].astype(jnp.float32) + added).astype(jnp.bfloat16)

    def attend(s, combine):
        if s == 1:
            values(s)
        arrive(k_ref.at[s, 1], arrival(("k", s)))
        for n in range(4):
            score(s, n)
        if s == 0:
            values(s)
        arrive(v_ref.at[s, 1], arrival(("v", s)))
        spreads = []
        for n in range(4):
            mix(s, n)
            spreads.append(Spread(("a", s, n), "zx" if n % 2 else "xz", att_region(s, n)))
            spreads[-1].start()
        drip(2)
        await_projection(s)
        for n in range(4):
            spreads[n].stage(0)
            drip(1)
        for n in range(4):
            spreads[n].stage(1)
            span = block_of(n)
            lhs = jnp.concatenate([attg[s, i, span, :] for i in range(4)], axis=1)
            send_part[s, span, :] = jnp.dot(lhs, wo[s, 1 - y], preferred_element_type=jnp.float32).astype(jnp.bfloat16)
            push(
                send_part.at[s, strip(n), :], recv_part.at[s, strip(n), :], arrival(("p", s, n)), partner["y"]
            )
            own_part[span, :] = jnp.dot(lhs, wo[s, y], preferred_element_type=jnp.float32)
            drip(1)
            if n:
                combine(n - 1)
        combine(3)

    normalize(lambda n, span: xg[n, span, :], wide, 2, 0, 0, 4 * rows)
    every = slice(0, 4 * rows)
    k_ref[0, 0] = project(0, KEY, every)
    swap(0, k_ref, "k")
    q_ref[...] = project(0, QUERY, every)
    rest_copy.wait()
    ms = [
        Spread(
            ("m", n), "zyx" if n == 1 else "zxy",
            lambda xx, yy, zz, n=n: midg.at[4 * yy + 2 * zz + xx, strip(n), :],
        )
        for n in range(4)
    ]

    def middle(n):
        midg[pair, block_of(n), :] = total_of(0, n, rest)
        ms[n].start()
        drip(1)

    attend(0, middle)
    for m in ms:
        m.stage(0)
        drip(1)
    for m in ms:
        m.stage(1)
        drip(2)
    drip(len(later))
    for part in (KEY, QUERY):
        for b in (zh, 1 - zh):
            await_weights(1, part, b)
    for n in range(4):
        ms[n].stage(2)
        normalize(lambda i, at: midg[i, at, :], PAIR, 8, 1, n * rows, rows)
        k_ref[1, 0, block_of(n), :] = project(1, KEY, block_of(n), False)
        q_ref[block_of(n), :] = project(1, QUERY, block_of(n), False)
    swap(1, k_ref, "k")

    block = pl.ds(pl.multiple_of(tile * rows, rows), rows)
    outs = []

    def first_output():
        for i in range(4):
            src, dst = midg.at[4 * y + i, block, :], out.at[zh, :, pl.ds(i * PAIR, PAIR)]
            outs.append(pltpu.make_async_copy(src, dst, loc.at[2 + i]))
            push(src, dst, arrival("mid"), dev(0, x, y, over), core == 1)

        @pl.when(core == 0)
        def _():
            for copy in outs:
                copy.start()

    def last(n):
        fin[block_of(n), :] = total_of(1, n, midg.at[pair])
        push(
            fin.at[strip(n), :], out.at[zh, :, pl.ds(pl.multiple_of(tile * PAIR, PAIR), PAIR)],
            f_sem.at[zh], dev(1, n % 2, y, 2 * half + n // 2),
        )

    first_output()
    attend(1, last)

    @pl.when(core == 0)
    def _():
        for copy in outs:
            copy.wait()
        arrive(out.at[1 - zh], arrival("mid"))

    @pl.when(core == 1)
    def _():
        for m in range(2):
            arrive(out.at[m], f_sem.at[m])

    for copy, when in sent:
        if when is None:
            copy.wait_send()
        else:
            pl.when(when)(copy.wait_send)


def local_cubes(feats, gain, w_qkv, w_out, block_mask):
    dma = pltpu.SemaphoreType.DMA
    bf, f32 = jnp.bfloat16, jnp.float32
    rows, wide = feats.shape[1], feats.shape[2]
    mine, whole = 4 * rows, 2 * wide
    vmem = pltpu.VMEM
    return pl.pallas_call(
        relay_kernel,
        out_shape=jax.ShapeDtypeStruct(feats.shape, bf),
        in_specs=[ANY] * 4 + [pl.BlockSpec(memory_space=pltpu.SMEM)],
        out_specs=ANY,
        scratch_shapes=[
            vmem((2, mine, wide), bf), vmem((2, mine, wide), bf), vmem((2, 1, whole), f32),
            vmem((2, 3, 2, wide, PAIR), bf), vmem((2, 2, wide, PAIR), bf),
            vmem((mine, PAIR), bf), vmem((2, 2, mine, PAIR), bf), vmem((2, 2, mine, PAIR), bf),
            vmem((4, 2, rows, 4 * HD), bf), vmem((4, 2, rows, HD), f32),
            vmem((2, 4, mine, PAIR), bf), vmem((mine, PAIR), f32),
            vmem((2, mine, PAIR), bf), vmem((2, mine, PAIR), bf),
            vmem((mine, PAIR), bf), vmem((8, mine, PAIR), bf), vmem((mine, PAIR), bf),
            dma((160,)), dma((110,)), dma((2, 3, 2)), dma((2, 2)), dma((2,)), dma((6,)),
        ],
        compiler_params=pltpu.CompilerParams(
            collective_id=0, has_side_effects=True, vmem_limit_bytes=63 * 2**20
        ),
        name="relay",
    )(feats, gain, w_qkv, w_out, block_mask)[None]


def solution(mesh):
    cubes = (mesh.shape["pipe"], mesh.shape["node"], mesh.shape["head"]) == (2, 8, 2)
    return jax.shard_map(
        local_cubes if cubes else local_any,
        mesh=mesh,
        in_specs=(
            P(None, "node", "head"),
            P("pipe", None),
            P("pipe", None, "node", "head"),
            P("pipe", "head", "node"),
            P(),
        ),
        out_specs=P("pipe", None, "node", "head"),
        check_vma=False,
    )
```
